128 devices in a mesh: row: 8 (over y_hi, z), col: 16 (over y_lo, x, core).
Axes of the slice: x: 4, y: 4 (y_hi: 2, y_lo: 2; y = y_hi * 2 + y_lo), z: 4, core: 2. Of those that a mesh axis runs over, the one named last changes fastest.
Arguments:
- a_tiles: float32 [8, 16, 8, 128, 128], P('row', 'col'), may hold values from -6 to 6
- b_tiles: float32 [8, 16, 8, 128, 128], P('row', 'col'), may hold values from -0.25 to 0.25
- pair_lists: int32 [8, 16, 16, 3, 32], P('row', 'col'), may hold values from 0 to 63, as said below
- stack_counts: int32 [8, 16, 16], P('row', 'col'), may hold values from 1 to 32, as said below
Outputs:
- c_tiles: float32 [8, 16, 32, 128, 128], P('row', 'col')
The draws below stay inside these ranges and needn't reach their ends.
Inputs may be any that keep to these rules, and one draw needn't show every extreme that they name: `pair_lists`: entry 0 of a list column is an A tile slot below 8, entry 1 a tile of bcol below 64, entry 2 a product tile below 32; entries past the live count are valid indices that do not count. `stack_counts`: live entries of each list; in every draw some list has all 32 live.
All inputs are finite; a program needn't handle non-finite values.
Results may differ from the reference program's by a relative error of at most 0.0003.
Values sent between devices are 32-bit elements; how exact they have to be, the bound alone decides.
No kernel may reach another device: no remote copies, remote signals or barrier semaphores. Data moves between devices by JAX's collectives and lax.ppermute only.
A program may use at most 64 MiB of HBM per device.

```python
import jax
import jax.numpy as jnp
from jax import lax

BLK = 128
ASLOT = 8
BSLOT = 8
CT = 32
PAIRS = 32
N_ROW = 8
N_COL = 16


def draw_pair_lists(key, part):
    key_a, key_b, key_c = jax.random.split(jax.random.fold_in(key, 11), 3)
    shape = (N_ROW, N_COL, N_COL, 1, PAIRS)
    a_part = jax.random.randint(key_a, shape, 0, ASLOT, dtype=jnp.int32)
    b_part = jax.random.randint(key_b, shape, 0, N_ROW * BSLOT, dtype=jnp.int32)
    c_part = jax.random.randint(key_c, shape, 0, CT, dtype=jnp.int32)
    return jnp.concatenate([a_part, b_part, c_part], axis=3)


def draw_stack_counts(key, part):
    key_level, key_jitter, key_pick = jax.random.split(jax.random.fold_in(key, 23), 3)
    ninth = max(PAIRS // 9, 1)
    level = jax.random.randint(key_level, (N_ROW, N_COL, 1), 0, 4, dtype=jnp.int32)
    jitter = jax.random.randint(key_jitter, (N_ROW, N_COL, N_COL), 0, ninth, dtype=jnp.int32)
    counts = jnp.minimum(1 + level * level * ninth + jitter, PAIRS)
    total_lists = N_ROW * N_COL * N_COL
    picked = jax.random.randint(key_pick, (), 0, total_lists, dtype=jnp.int32)
    flat_ids = jnp.arange(total_lists, dtype=jnp.int32).reshape(N_ROW, N_COL, N_COL)
    return jnp.where(flat_ids == picked, PAIRS, counts).astype(jnp.int32)


def levels(key, dims, cuts, smallest, largest):
    def one(dim, blocks):
        draws = jax.random.uniform(jax.random.fold_in(jax.random.fold_in(key, 6), dim), (blocks,), jnp.float32, smallest / len(cuts), largest / len(cuts))
        return jnp.repeat(jnp.exp(draws), dims[dim] // blocks).reshape((-1,) + (1,) * (len(dims) - dim - 1))

    level = one(*cuts[0])
    for cut in cuts[1:]:
        level = level * one(*cut)
    return level


def bell_draw(own_key, dims, spread, limit, shards=(), kind=jnp.bfloat16):
    values = jax.random.normal(own_key, dims, jnp.float32) * spread
    if len(shards) > 0:
        values = levels(own_key, dims, shards, -0.22, 0.18) * values
    return jnp.clip(values, min=-limit, max=limit).astype(kind)


def setup_inputs(seed: int = 0) -> dict:
    seeds = jax.random.split(jax.random.key(seed), 5)
    return {
        "a_tiles": bell_draw(seeds[0], (N_ROW, N_COL, ASLOT, BLK, BLK), 1.0, 6.0, ((0, 8), (1, 16)), jnp.float32),
        "b_tiles": bell_draw(seeds[1], (N_ROW, N_COL, BSLOT, BLK, BLK), (4 * BLK) ** -0.5, 0.25, ((0, 8), (1, 16)), jnp.float32),
        "pair_lists": draw_pair_lists(jax.random.fold_in(seeds[4], 71), 0),
        "stack_counts": draw_stack_counts(jax.random.fold_in(seeds[4], 71), 0),
    }


def reference(a_tiles, b_tiles, pair_lists, stack_counts):
    def one_device(flat_index):
        grid_row = flat_index // N_COL
        grid_col = flat_index % N_COL
        a_row = lax.dynamic_index_in_dim(a_tiles, grid_row, 0, keepdims=False)
        b_column = lax.dynamic_index_in_dim(b_tiles, grid_col, 1, keepdims=False)
        b_column = b_column.reshape(N_ROW * BSLOT, BLK, BLK)
        lists_here = lax.dynamic_index_in_dim(lax.dynamic_index_in_dim(pair_lists, grid_row, 0, keepdims=False), grid_col, 0, keepdims=False)
        counts_here = lax.dynamic_index_in_dim(lax.dynamic_index_in_dim(stack_counts, grid_row, 0, keepdims=False), grid_col, 0, keepdims=False)

        def per_panel(totals, panel_index):
            a_panel = lax.dynamic_index_in_dim(a_row, panel_index, 0, keepdims=False)
            stack_list = lax.dynamic_index_in_dim(lists_here, panel_index, 0, keepdims=False)
            count_live = lax.dynamic_index_in_dim(counts_here, panel_index, 0, keepdims=False)
            left_tiles = jnp.take(a_panel, stack_list[0], axis=0)
            right_tiles = jnp.take(b_column, stack_list[1], axis=0)
            products = jnp.einsum("gij,gjk->gik", left_tiles, right_tiles, precision=lax.Precision.HIGHEST, preferred_element_type=jnp.float32)
            is_live = jnp.arange(PAIRS, dtype=jnp.int32) < count_live
            products = jnp.where(is_live[:, None, None], products, jnp.zeros_like(products))
            return totals.at[stack_list[2]].add(products), None

        start_totals = jnp.zeros((CT, BLK, BLK), jnp.float32)
        totals, unused = lax.scan(per_panel, start_totals, jnp.arange(N_COL, dtype=jnp.int32))
        return totals

    result = lax.map(one_device, jnp.arange(N_ROW * N_COL, dtype=jnp.int32))
    return result.reshape(N_ROW, N_COL, CT, BLK, BLK)
```

```python
import functools

import jax
import jax.numpy as jnp
from jax import lax
from jax.experimental import pallas as pl
from jax.experimental.pallas import tpu as pltpu
from jax.sharding import PartitionSpec as P

CT = 32
BIG = 32
SMALL = 8
CLASSES = 3
LIST = 512 + SMALL
COUNTS = 4 * LIST
A_SLOTS = 128
ZERO_SLOT = A_SLOTS
B_SLOTS = 64
BF = jnp.bfloat16
F32 = jnp.float32


def move_a(value, dy=0, dx=0, dc=0):
    pairs = []
    for i in range(16):
        y, x, c = i // 8, (i // 2) % 4, i % 2
        pairs.append((i, ((y + dy) % 2) * 8 + ((x + dx) % 4) * 2 + (c + dc) % 2))
    return lax.ppermute(value, "col", pairs)


def move_b(value, dy=0, dz=0):
    pairs = []
    for i in range(8):
        y, z = i // 4, i % 4
        pairs.append((i, ((y + dy) % 2) * 4 + (z + dz) % 4))
    return lax.ppermute(value, "row", pairs)


def a_slot(dy, dx, dc):
    return ((dy * 4 + dx) * 2 + dc) * 8


def b_slot(dy, dz):
    return (dy * 4 + dz) * 8


def stage_a(dy, dx):
    return jnp.where((dy == 0) & (dx != 2), 0, jnp.where((dx == 0) | (dy == 0), 1, 2))


def stage_b(dy, dz):
    return jnp.where(dz == 2, 1 + dy, jnp.where((dy == 1) & (dz != 0), 1, 0))


def packed_entries(lists, counts):
    q = lax.axis_index("col")
    r = lax.axis_index("row")
    j = jnp.arange(16, dtype=jnp.int32)[:, None]
    dy, dx, dc = (j // 8) ^ (q // 8), ((j // 2) - (q // 2)) & 3, (j & 1) ^ (q & 1)
    a, b, m = lists[:, 0], lists[:, 1], lists[:, 2]
    part = b >> 3
    by, bz = (part >> 2) ^ (r >> 2), (part - r) & 3
    stage = jnp.maximum(stage_a(dy, dx), stage_b(by, bz))
    live = jnp.arange(32, dtype=jnp.int32)[None, :] < counts[:, None]
    stage = jnp.where(live, stage, CLASSES)
    slot_a = ((dy * 4 + dx) * 2 + dc) * 8 + a
    slot_b = (by * 4 + bz) * 8 + (b & 7)
    return (slot_a | (slot_b << 8) | (m << 14) | (stage << 19)).reshape(-1)


def halves(v):
    hi = v.astype(BF)
    return hi, (v - hi.astype(F32)).astype(BF)


def split_tiles(src, start, count, dst, base):
    def one(i, carry):
        hi, lo = halves(src[start + i])
        dst[base + i, :, :128] = hi
        dst[base + i, :, 128:] = lo
        return carry

    lax.fori_loop(0, count, one, 0, unroll=4)


def prepare_kernel(w_ref, a_ref, b_ref, l_ref, sa, sb, c_ref):
    split_tiles(a_ref, 0, 8, sa, 0)
    split_tiles(b_ref, 0, 8, sb, 0)
    sa[ZERO_SLOT] = jnp.zeros(sa.shape[1:], BF)
    c_ref[...] = jnp.zeros_like(c_ref)

    def step(e, ns):
        w = w_ref[e]
        c = w >> 19
        pos = jnp.where(c == 0, ns[0], jnp.where(c == 1, ns[1], jnp.where(c == 2, ns[2], ns[3])))
        l_ref[pos] = w & 0x7FFFF
        return tuple(ns[k] + (c == k).astype(jnp.int32) for k in range(4))

    start = tuple(jnp.int32(k * LIST) for k in range(4))
    ends = lax.fori_loop(0, 512, step, start, unroll=8)
    for k in range(CLASSES):
        for u in range(SMALL):
            l_ref[ends[k] + u] = jnp.int32(ZERO_SLOT)
        l_ref[COUNTS + k] = ends[k] - k * LIST


STATE = (
    ((A_SLOTS + 1, 128, 256), BF),
    ((B_SLOTS, 128, 256), BF),
    ((CT, 128, 128), F32),
)


def prepare(words, a, b):
    vmem = pl.BlockSpec(memory_space=pltpu.VMEM)
    smem = pl.BlockSpec(memory_space=pltpu.SMEM)
    return pl.pallas_call(
        prepare_kernel,
        out_shape=(jax.ShapeDtypeStruct((COUNTS + CLASSES,), jnp.int32),) + tuple(pltpu.VMEM(*s) for s in STATE),
        in_specs=[smem, vmem, vmem],
        out_specs=(smem, vmem, vmem, vmem),
        name="prepare",
        compiler_params=pltpu.CompilerParams(vmem_limit_bytes=8 * 1024 * 1024),
        cost_estimate=pl.CostEstimate(flops=0, bytes_accessed=16_000_000, transcendentals=0),
    )(words, a, b)


def products_kernel(stage, a_parts, b_parts, n_in, *refs):
    l_ref = refs[0]
    new = refs[1 : 1 + n_in]
    sa_in, sb_in, c_in = refs[1 + n_in : 4 + n_in]
    if stage < CLASSES - 1:
        sa, sb, c_ref = refs[4 + n_in :]
    else:
        sa, sb, c_ref = sa_in, sb_in, refs[4 + n_in]
        sa, sb = refs[5 + n_in :]
        c_ref[...] = c_in[...]
    for k, start, count, base in a_parts:
        split_tiles(new[k], start, count, sa, base)
    for k, start, count, base in b_parts:
        split_tiles(new[k], start, count, sb, base)

    def group(size, first):
        sums, places = [], []
        for u in range(size):
            w = l_ref[first + u]
            right = sb[(w >> 8) & 0x3F]
            r = jnp.dot(sa[w & 0xFF], jnp.concatenate([right, right], axis=0), preferred_element_type=F32)
            sums.append(r[:, :128] + r[:, 128:])
            places.append(w >> 14)
        for s, m in zip(sums, places):
            c_ref[m] = c_ref[m] + s

    base = stage * LIST
    count = l_ref[COUNTS + stage]
    bigs = count // BIG
    rest = (count - bigs * BIG + SMALL - 1) // SMALL

    def big(g, carry):
        group(BIG, base + g * BIG)
        return carry

    def small(g, carry):
        group(SMALL, base + bigs * BIG + g * SMALL)
        return carry

    lax.fori_loop(0, bigs, big, 0)
    lax.fori_loop(0, rest, small, 0)


def products(stage, entries, news, a_parts, b_parts, state, micros):
    n_in = len(news)
    vmem = pl.BlockSpec(memory_space=pltpu.VMEM)
    smem = pl.BlockSpec(memory_space=pltpu.SMEM)
    state = tuple(pltpu.with_memory_space_constraint(s, pltpu.VMEM) for s in state)
    last = stage == CLASSES - 1
    outs = [pltpu.VMEM(*s) for s in STATE]
    aliases = {1 + n_in + i: i for i in range(3)}
    if last:
        outs = [jax.ShapeDtypeStruct(*STATE[2])] + outs[:2]
        aliases = {1 + n_in: 1, 2 + n_in: 2}
    return pl.pallas_call(
        functools.partial(products_kernel, stage, a_parts, b_parts, n_in),
        out_shape=tuple(outs),
        in_specs=[smem] + [vmem] * (n_in + 3),
        out_specs=(vmem,) * 3,
        input_output_aliases=aliases,
        name=f"products_{stage}",
        compiler_params=pltpu.CompilerParams(vmem_limit_bytes=12 * 1024 * 1024),
        cost_estimate=pl.CostEstimate(flops=0, bytes_accessed=micros * 3_000_000, transcendentals=0),
    )(entries, *news, *state)


def after(value, *others):
    return lax.optimization_barrier((value,) + others)[0]


def body(a_tiles, b_tiles, pair_lists, stack_counts):
    a, b = a_tiles[0, 0], b_tiles[0, 0]
    b10, b03, b01 = move_b(b, dy=1), move_b(b, dz=1), move_b(b, dz=-1)
    a03, a01 = move_a(a, dx=1), move_a(a, dx=-1)
    a_late = after(a, b10)
    a10, s00 = move_a(a_late, dy=1), move_a(a_late, dc=1)
    words = packed_entries(pair_lists[0, 0], stack_counts[0, 0])
    entries, *state = prepare(words, a, b)
    a03, a01, b10, b03, b01, entries, *state = lax.optimization_barrier((a03, a01, b10, b03, b01, entries, *state))
    bp = move_b(jnp.concatenate([b10, b03[:4]]), dz=1)
    bm = move_b(jnp.concatenate([b10, b01[4:]]), dz=-1)
    a02p, a02m = move_a(a03[:4], dx=1), move_a(a01[4:], dx=-1)
    a03_late, a01_late, a02p, a02m = lax.optimization_barrier((a03, a01, a02p, a02m))
    s03, s01 = move_a(a03_late, dc=1), move_a(a01_late, dc=1)
    state = products(
        0,
        entries,
        (a03, a01, s00, s03, s01, b03, b01, b10),
        [(0, 0, 8, a_slot(0, 3, 0)), (1, 0, 8, a_slot(0, 1, 0)), (2, 0, 8, a_slot(0, 0, 1)), (3, 0, 8, a_slot(0, 3, 1)), (4, 0, 8, a_slot(0, 1, 1))],
        [(5, 0, 8, b_slot(0, 3)), (6, 0, 8, b_slot(0, 1)), (7, 0, 8, b_slot(1, 0))],
        state,
        8,
    )
    a13, a11 = move_a(a10, dx=1), move_a(a10, dx=-1)
    s10, s02p, s02m = move_a(a10, dc=1), move_a(a02p, dc=1), move_a(a02m, dc=1)
    bp, bm, a10, a02p, a02m, s10, s02p, s02m, *state = lax.optimization_barrier(
        (bp, bm, a10, a02p, a02m, s10, s02p, s02m, *state)
    )
    b12p, b12m = move_b(bp[:4], dz=1), move_b(bm[4:8], dz=-1)
    a12p, a12m = move_a(a13[:4], dx=1), move_a(a11[4:], dx=-1)
    s13, s11 = move_a(a13, dc=1), move_a(a11, dc=1)
    state = products(
        1,
        entries,
        (a10, a02p, a02m, s10, s02p, s02m, bp, bm),
        [
            (3 * c + k, 0, n, slot)
            for c in (0, 1)
            for k, n, slot in ((0, 8, a_slot(1, 0, c)), (1, 4, a_slot(0, 2, c)), (2, 4, a_slot(0, 2, c) + 4))
        ],
        [
            (6, 0, 8, b_slot(1, 3)),
            (6, 8, 4, b_slot(0, 2)),
            (7, 0, 8, b_slot(1, 1)),
            (7, 8, 4, b_slot(0, 2) + 4),
        ],
        state,
        10,
    )
    s12p, s12m = move_a(a12p, dc=1), move_a(a12m, dc=1)
    c = products(
        2,
        entries,
        (a13, a11, a12p, a12m, s13, s11, s12p, s12m, b12p, b12m),
        [
            (4 * c + k, 0, n, slot)
            for c in (0, 1)
            for k, n, slot in (
                (0, 8, a_slot(1, 3, c)),
                (1, 8, a_slot(1, 1, c)),
                (2, 4, a_slot(1, 2, c)),
                (3, 4, a_slot(1, 2, c) + 4),
            )
        ],
        [(8 + h, 0, 4, b_slot(1, 2) + 4 * h) for h in (0, 1)],
        state,
        10,
    )[0]
    return c[None, None]


def solution(mesh):
    return jax.shard_map(
        body,
        mesh=mesh,
        in_specs=(
            P("row", "col", None, None, None),
            P("row", "col", None, None, None),
            P("row", "col", None, None, None),
            P("row", "col", None),
        ),
        out_specs=P("row", "col", None, None, None),
        check_vma=False,
    )
```

```python
import functools

import jax
import jax.numpy as jnp
from jax import lax
from jax.experimental import pallas as pl
from jax.experimental.pallas import tpu as pltpu
from jax.sharding import PartitionSpec as P

CT = 32
BIG = 32
SMALL = 8
CLASSES = 5
LIST = 512 + SMALL
COUNTS = (CLASSES + 1) * LIST
A_SLOTS = 128
ZERO_SLOT = A_SLOTS
B_SLOTS = 64
BF = jnp.bfloat16
F32 = jnp.float32


def move_a(value, dy=0, dx=0, dc=0):
    pairs = []
    for i in range(16):
        y, x, c = i // 8, (i // 2) % 4, i % 2
        pairs.append((i, ((y + dy) % 2) * 8 + ((x + dx) % 4) * 2 + (c + dc) % 2))
    return lax.ppermute(value, "col", pairs)


def move_b(value, dy=0, dz=0):
    pairs = []
    for i in range(8):
        y, z = i // 4, i % 4
        pairs.append((i, ((y + dy) % 2) * 4 + (z + dz) % 4))
    return lax.ppermute(value, "row", pairs)


def a_slot(dy, dx, dc):
    return ((dy * 4 + dx) * 2 + dc) * 8


def b_slot(dy, dz):
    return (dy * 4 + dz) * 8


def stage_of(dy, dx, dc, by, bz):
    far_b = (by == 1) & (bz != 0)
    stage = jnp.where(far_b, 2, dc)
    stage = jnp.where(dx == 2, 3, stage)
    return jnp.where(far_b & (bz == 2), 4, stage)


def packed_entries(lists, counts):
    q = lax.axis_index("col")
    r = lax.axis_index("row")
    j = jnp.arange(16, dtype=jnp.int32)[:, None]
    dy, dx, dc = (j // 8) ^ (q // 8), ((j // 2) - (q // 2)) & 3, (j & 1) ^ (q & 1)
    a, b, m = lists[:, 0], lists[:, 1], lists[:, 2]
    part = b >> 3
    by, bz = (part >> 2) ^ (r >> 2), (part - r) & 3
    stage = stage_of(dy, dx, dc, by, bz)
    live = jnp.arange(32, dtype=jnp.int32)[None, :] < counts[:, None]
    stage = jnp.where(live, stage, CLASSES)
    slot_a = ((dy * 4 + dx) * 2 + dc) * 8 + a
    slot_b = (by * 4 + bz) * 8 + (b & 7)
    return (slot_a | (slot_b << 8) | (m << 14) | (stage << 19)).reshape(-1)


def halves(v):
    hi = v.astype(BF)
    return hi, (v - hi.astype(F32)).astype(BF)


def split_tiles(src, start, count, dst, base):
    def one(i, carry):
        hi, lo = halves(src[start + i])
        dst[base + i, :, :128] = hi
        dst[base + i, :, 128:] = lo
        return carry

    lax.fori_loop(0, count, one, 0, unroll=4)


def sort_kernel(w_ref, words_ref, l_ref, rank_ref, place_ref, counts, places, sems):
    kinds = jnp.broadcast_to(words_ref[...] >> 19, (8, 512))
    is_kind = kinds == lax.broadcasted_iota(jnp.int32, (8, 512), 0)
    before = lax.broadcasted_iota(jnp.int32, (512, 512), 0) <= lax.broadcasted_iota(jnp.int32, (512, 512), 1)
    ones = jnp.where(is_kind, 1.0, 0.0).astype(BF)
    triangle = jnp.where(before, 1.0, 0.0).astype(BF)
    rank = jnp.dot(ones, triangle, preferred_element_type=F32).astype(jnp.int32)
    rank_ref[...] = rank
    starts = lax.broadcasted_iota(jnp.int32, (8, 512), 0) * LIST
    place_ref[...] = jnp.sum(jnp.where(is_kind, starts + rank - 1, 0), axis=0, keepdims=True)
    copies = [
        pltpu.make_async_copy(rank_ref, counts, sems.at[0]),
        pltpu.make_async_copy(place_ref, places, sems.at[1]),
    ]
    for copy in copies:
        copy.start()
    for copy in copies:
        copy.wait()

    def store(e, carry):
        l_ref[places[0, e]] = w_ref[e] & 0x7FFFF
        return carry

    lax.fori_loop(0, 512, store, 0, unroll=16)
    for k in range(CLASSES):
        count = counts[k, 511]
        for u in range(SMALL):
            l_ref[k * LIST + count + u] = jnp.int32(ZERO_SLOT)
        l_ref[COUNTS + k] = count


def sort_entries(words):
    smem = pl.BlockSpec(memory_space=pltpu.SMEM)
    return pl.pallas_call(
        sort_kernel,
        out_shape=jax.ShapeDtypeStruct((COUNTS + CLASSES,), jnp.int32),
        in_specs=[smem, pl.BlockSpec(memory_space=pltpu.VMEM)],
        out_specs=smem,
        scratch_shapes=[
            pltpu.VMEM((8, 512), jnp.int32),
            pltpu.VMEM((1, 512), jnp.int32),
            pltpu.SMEM((8, 512), jnp.int32),
            pltpu.SMEM((1, 512), jnp.int32),
            pltpu.SemaphoreType.DMA((2,)),
        ],
        name="sort_entries",
        cost_estimate=pl.CostEstimate(flops=0, bytes_accessed=16_000_000, transcendentals=0),
    )(words, words.reshape(1, 512))


STATE = (
    ((A_SLOTS + 1, 128, 256), BF),
    ((B_SLOTS, 128, 256), BF),
    ((CT, 128, 128), F32),
)


def split_kernel(n_in, a_parts, b_parts, *refs):
    news, (sa, sb, c_ref) = refs[:n_in], refs[n_in : n_in + 3]
    a_hbm, b_hbm = news[:2]
    a_ref, b_ref, sems = refs[n_in + 3 :]
    copies = [
        pltpu.make_async_copy(a_hbm, a_ref, sems.at[0]),
        pltpu.make_async_copy(b_hbm, b_ref, sems.at[1]),
    ]
    for copy in copies:
        copy.start()
    sa[ZERO_SLOT] = jnp.zeros(sa.shape[1:], BF)
    c_ref[...] = jnp.zeros_like(c_ref)
    for k, start, count, base in a_parts:
        split_tiles(news[k], start, count, sa, base)
    for k, start, count, base in b_parts:
        split_tiles(news[k], start, count, sb, base)
    for copy in copies:
        copy.wait()
    split_tiles(a_ref, 0, 8, sa, a_slot(0, 0, 0))
    split_tiles(b_ref, 0, 8, sb, b_slot(0, 0))


def first_splits(news, a_parts, b_parts):
    vmem = pl.BlockSpec(memory_space=pltpu.VMEM)
    hbm = pl.BlockSpec(memory_space=pl.ANY)
    own = tuple(pltpu.with_memory_space_constraint(v, pltpu.HBM) for v in news[:2])
    return pl.pallas_call(
        functools.partial(split_kernel, len(news), a_parts, b_parts),
        out_shape=tuple(pltpu.VMEM(*s) for s in STATE),
        in_specs=[hbm] * 2 + [vmem] * (len(news) - 2),
        out_specs=(vmem,) * 3,
        scratch_shapes=[pltpu.VMEM((8, 128, 128), F32)] * 2 + [pltpu.SemaphoreType.DMA((2,))],
        name="first_splits",
        compiler_params=pltpu.CompilerParams(vmem_limit_bytes=8 * 1024 * 1024),
        cost_estimate=pl.CostEstimate(flops=0, bytes_accessed=4_000_000, transcendentals=0),
    )(*own, *news[2:])


def more_splits_kernel(n_in, a_parts, b_parts, *refs):
    news, (sa, sb) = refs[:n_in], refs[n_in + 2 :]
    for k, start, count, base in a_parts:
        split_tiles(news[k], start, count, sa, base)
    for k, start, count, base in b_parts:
        split_tiles(news[k], start, count, sb, base)


def more_splits(news, a_parts, b_parts, state):
    vmem = pl.BlockSpec(memory_space=pltpu.VMEM)
    tiles = tuple(pltpu.with_memory_space_constraint(s, pltpu.VMEM) for s in state[:2])
    news = tuple(pltpu.with_memory_space_constraint(s, pltpu.VMEM) for s in news)
    sa, sb = pl.pallas_call(
        functools.partial(more_splits_kernel, len(news), a_parts, b_parts),
        out_shape=tuple(pltpu.VMEM(*s) for s in STATE[:2]),
        in_specs=[vmem] * (len(news) + 2),
        out_specs=(vmem,) * 2,
        input_output_aliases={len(news) + i: i for i in range(2)},
        name="more_splits",
        compiler_params=pltpu.CompilerParams(vmem_limit_bytes=8 * 1024 * 1024),
        cost_estimate=pl.CostEstimate(flops=0, bytes_accessed=4_000_000, transcendentals=0),
    )(*news, *tiles)
    return sa, sb, state[2]


def products_kernel(stage, a_parts, b_parts, n_in, *refs):
    l_ref = refs[0]
    new = refs[1 : 1 + n_in]
    sa_in, sb_in, c_in = refs[1 + n_in : 4 + n_in]
    sa, sb, c_ref = refs[4 + n_in : 7 + n_in]
    for k, start, count, base in a_parts:
        split_tiles(new[k], start, count, sa, base)
    for k, start, count, base in b_parts:
        split_tiles(new[k], start, count, sb, base)

    def group(size, first):
        sums, places = [], []
        for u in range(size):
            w = l_ref[first + u]
            right = sb[(w >> 8) & 0x3F]
            r = jnp.dot(sa[w & 0xFF], jnp.concatenate([right, right], axis=0), preferred_element_type=F32)
            sums.append(r[:, :128] + r[:, 128:])
            places.append(w >> 14)
        for s, m in zip(sums, places):
            c_ref[m] = c_ref[m] + s

    base = stage * LIST
    count = l_ref[COUNTS + stage]
    bigs = count // BIG
    rest = (count - bigs * BIG + SMALL - 1) // SMALL

    def big(g, carry):
        group(BIG, base + g * BIG)
        return carry

    def small(g, carry):
        group(SMALL, base + bigs * BIG + g * SMALL)
        return carry

    lax.fori_loop(0, bigs, big, 0)
    lax.fori_loop(0, rest, small, 0)
    if stage == CLASSES - 1:
        out_hbm, sem = refs[7 + n_in :]
        copy = pltpu.make_async_copy(c_ref, out_hbm, sem)
        copy.start()
        copy.wait()


def products(stage, entries, news, a_parts, b_parts, state, micros):
    n_in = len(news)
    vmem = pl.BlockSpec(memory_space=pltpu.VMEM)
    smem = pl.BlockSpec(memory_space=pltpu.SMEM)
    state = tuple(pltpu.with_memory_space_constraint(s, pltpu.VMEM) for s in state)
    news = tuple(pltpu.with_memory_space_constraint(s, pltpu.VMEM) for s in news)
    last = stage == CLASSES - 1
    outs = [pltpu.VMEM(*s) for s in STATE]
    aliases = {1 + n_in + i: i for i in range(3)}
    out_specs, scratch = (vmem,) * 3, []
    if last:
        outs += [pltpu.HBM(*STATE[2])]
        out_specs += (pl.BlockSpec(memory_space=pltpu.HBM),)
        scratch = [pltpu.SemaphoreType.DMA(())]
    return pl.pallas_call(
        functools.partial(products_kernel, stage, a_parts, b_parts, n_in),
        out_shape=tuple(outs),
        in_specs=[smem] + [vmem] * (n_in + 3),
        out_specs=out_specs,
        scratch_shapes=scratch,
        input_output_aliases=aliases,
        name=f"products_{stage}",
        compiler_params=pltpu.CompilerParams(vmem_limit_bytes=12 * 1024 * 1024),
        cost_estimate=pl.CostEstimate(flops=5 * 10**10, bytes_accessed=1, transcendentals=0),
    )(entries, *news, *state)


def body(a_tiles, b_tiles, pair_lists, stack_counts):
    barrier = lax.optimization_barrier
    a, b = a_tiles[0, 0], b_tiles[0, 0]
    a10, a03, a01 = move_a(a, dy=1), move_a(a, dx=1), move_a(a, dx=-1)
    words = packed_entries(pair_lists[0, 0], stack_counts[0, 0])
    words, b_late = barrier((words, b))
    b03, b01 = move_b(b_late, dz=1), move_b(b_late, dz=-1)
    entries = sort_entries(words)
    a10, a03, a01, entries, a, b = barrier((a10, a03, a01, entries, a, b))
    b10 = move_b(b, dy=1)
    a13, a11 = move_a(a10, dx=1), move_a(a10, dx=-1)
    state = first_splits(
        (a, b, a10, a03, a01),
        [(2, 0, 8, a_slot(1, 0, 0)), (3, 0, 8, a_slot(0, 3, 0)), (4, 0, 8, a_slot(0, 1, 0))],
        [],
    )
    b03, b01, *state = barrier((b03, b01, *state))
    b02p, b02m = move_b(b03[:4], dz=1), move_b(b01[4:], dz=-1)
    b10, b02p, b02m = barrier((b10, b02p, b02m))
    b13, b11 = move_b(b10, dz=1), move_b(b10, dz=-1)
    state = more_splits(
        (a13, a11, b03, b01, b10, b02p, b02m),
        [(0, 0, 8, a_slot(1, 3, 0)), (1, 0, 8, a_slot(1, 1, 0))],
        [
            (2, 0, 8, b_slot(0, 3)),
            (3, 0, 8, b_slot(0, 1)),
            (4, 0, 8, b_slot(1, 0)),
            (5, 0, 4, b_slot(0, 2)),
            (6, 0, 4, b_slot(0, 2) + 4),
        ],
        state,
    )
    a, a10, a03, a01, a13, a11, *state = barrier((a, a10, a03, a01, a13, a11, *state))
    ap = move_a(jnp.concatenate([a03[:4], a13[:4]]), dx=1)
    am = move_a(jnp.concatenate([a01[4:], a11[4:]]), dx=-1)
    near = move_a(jnp.concatenate([a, a10, a03, a01, a13, a11]), dc=1)
    state = products(0, entries, (), [], [], state, 3)
    state = products(
        1,
        entries,
        (near,),
        [
            (0, 8 * k, 8, a_slot(dy, dx, 1))
            for k, (dy, dx) in enumerate(((0, 0), (1, 0), (0, 3), (0, 1), (1, 3), (1, 1)))
        ],
        [],
        state,
        4,
    )
    b13, b11, *state = barrier((b13, b11, *state))
    b12p, b12m = move_b(b13[:4], dz=1), move_b(b11[4:], dz=-1)
    ap, am, b13, b11 = barrier((ap, am, b13, b11))
    far = move_a(jnp.concatenate([ap, am]), dc=1)
    state = products(
        2,
        entries,
        (ap, am, b13, b11),
        [(h, 4 * dy, 4, a_slot(dy, 2, 0) + 4 * h) for h in (0, 1) for dy in (0, 1)],
        [(2, 0, 8, b_slot(1, 3)), (3, 0, 8, b_slot(1, 1))],
        state,
        3,
    )
    state = products(
        3,
        entries,
        (far,),
        [(0, 8 * h + 4 * dy, 4, a_slot(dy, 2, 1) + 4 * h) for h in (0, 1) for dy in (0, 1)],
        [],
        state,
        3,
    )
    c = products(
        4,
        entries,
        (b12p, b12m),
        [],
        [(h, 0, 4, b_slot(1, 2) + 4 * h) for h in (0, 1)],
        state,
        2,
    )[3]
    return c[None, None]


def solution(mesh):
    return jax.shard_map(
        body,
        mesh=mesh,
        in_specs=(
            P("row", "col", None, None, None),
            P("row", "col", None, None, None),
            P("row", "col", None, None, None),
            P("row", "col", None),
        ),
        out_specs=P("row", "col", None, None, None),
        check_vma=False,
    )
```

```python
import functools

import jax
import jax.numpy as jnp
from jax import lax
from jax.experimental import pallas as pl
from jax.experimental.pallas import tpu as pltpu
from jax.sharding import PartitionSpec as P

CT = 32
GROUPS = (64, 32, 16, 8)
SMALL = 8
CLASSES = 5
LIST = 512 + SMALL
COUNTS = (CLASSES + 1) * LIST
A_SLOTS = 128
ZERO_SLOT = A_SLOTS
B_SLOTS = 64
BF = jnp.bfloat16
F32 = jnp.float32


def move_a(value, dy=0, dx=0, dc=0):
    pairs = []
    for i in range(16):
        y, x, c = i // 8, (i // 2) % 4, i % 2
        pairs.append((i, ((y + dy) % 2) * 8 + ((x + dx) % 4) * 2 + (c + dc) % 2))
    return lax.ppermute(value, "col", pairs)


def move_b(value, dy=0, dz=0):
    pairs = []
    for i in range(8):
        y, z = i // 4, i % 4
        pairs.append((i, ((y + dy) % 2) * 4 + (z + dz) % 4))
    return lax.ppermute(value, "row", pairs)


def a_slot(dy, dx, dc):
    return ((dy * 4 + dx) * 2 + dc) * 8


def b_slot(dy, dz):
    return (dy * 4 + dz) * 8


def stage_of(dy, dx, dc, by, bz):
    far_b = (by == 1) & (bz != 0)
    stage = jnp.where(far_b, 2, dc)
    stage = jnp.where(dx == 2, 3, stage)
    return jnp.where(far_b & (bz == 2), 4, stage)


def packed_entries(lists, counts):
    q = lax.axis_index("col")
    r = lax.axis_index("row")
    j = jnp.arange(16, dtype=jnp.int32)[:, None]
    dy, dx, dc = (j // 8) ^ (q // 8), ((j // 2) - (q // 2)) & 3, (j & 1) ^ (q & 1)
    a, b, m = lists[:, 0], lists[:, 1], lists[:, 2]
    part = b >> 3
    by, bz = (part >> 2) ^ (r >> 2), (part - r) & 3
    stage = stage_of(dy, dx, dc, by, bz)
    live = jnp.arange(32, dtype=jnp.int32)[None, :] < counts[:, None]
    stage = jnp.where(live, stage, CLASSES)
    slot_a = ((dy * 4 + dx) * 2 + dc) * 8 + a
    slot_b = (by * 4 + bz) * 8 + (b & 7)
    return (slot_a | (slot_b << 8) | (m << 14) | (stage << 19)).reshape(-1)


def halves(v):
    hi = v.astype(BF)
    return hi, (v - hi.astype(F32)).astype(BF)


def split_tiles(src, start, count, dst, base):
    def one(i, carry):
        hi, lo = halves(src[start + i])
        dst[base + i, :, :128] = hi
        dst[base + i, :, 128:] = lo
        return carry

    lax.fori_loop(0, count, one, 0, unroll=4)


def sort_kernel(w_ref, words_ref, l_ref, rank_ref, place_ref, counts, places, sems):
    kinds = jnp.broadcast_to(words_ref[...] >> 19, (8, 512))
    is_kind = kinds == lax.broadcasted_iota(jnp.int32, (8, 512), 0)
    before = lax.broadcasted_iota(jnp.int32, (512, 512), 0) <= lax.broadcasted_iota(jnp.int32, (512, 512), 1)
    ones = jnp.where(is_kind, 1.0, 0.0).astype(BF)
    triangle = jnp.where(before, 1.0, 0.0).astype(BF)
    rank = jnp.dot(ones, triangle, preferred_element_type=F32).astype(jnp.int32)
    rank_ref[...] = rank
    starts = lax.broadcasted_iota(jnp.int32, (8, 512), 0) * LIST
    place_ref[...] = jnp.sum(jnp.where(is_kind, starts + rank - 1, 0), axis=0, keepdims=True)
    copies = [
        pltpu.make_async_copy(rank_ref, counts, sems.at[0]),
        pltpu.make_async_copy(place_ref, places, sems.at[1]),
    ]
    for copy in copies:
        copy.start()
    for copy in copies:
        copy.wait()

    def store(e, carry):
        l_ref[places[0, e]] = w_ref[e] & 0x7FFFF
        return carry

    lax.fori_loop(0, 512, store, 0, unroll=16)
    for k in range(CLASSES):
        count = counts[k, 511]
        for u in range(SMALL):
            l_ref[k * LIST + count + u] = jnp.int32(ZERO_SLOT)
        l_ref[COUNTS + k] = count


def sort_entries(words):
    smem = pl.BlockSpec(memory_space=pltpu.SMEM)
    return pl.pallas_call(
        sort_kernel,
        out_shape=jax.ShapeDtypeStruct((COUNTS + CLASSES,), jnp.int32),
        in_specs=[smem, pl.BlockSpec(memory_space=pltpu.VMEM)],
        out_specs=smem,
        scratch_shapes=[
            pltpu.VMEM((8, 512), jnp.int32),
            pltpu.VMEM((1, 512), jnp.int32),
            pltpu.SMEM((8, 512), jnp.int32),
            pltpu.SMEM((1, 512), jnp.int32),
            pltpu.SemaphoreType.DMA((2,)),
        ],
        name="sort_entries",
        cost_estimate=pl.CostEstimate(flops=0, bytes_accessed=16_000_000, transcendentals=0),
    )(words, words.reshape(1, 512))


STATE = (
    ((A_SLOTS + 1, 128, 256), BF),
    ((B_SLOTS, 128, 256), BF),
    ((CT, 128, 128), F32),
)


def split_kernel(n_in, a_parts, b_parts, *refs):
    news, (sa, sb, c_ref) = refs[:n_in], refs[n_in : n_in + 3]
    a_hbm, b_hbm = news[:2]
    a_ref, b_ref, sems = refs[n_in + 3 :]
    copies = [
        pltpu.make_async_copy(a_hbm, a_ref, sems.at[0]),
        pltpu.make_async_copy(b_hbm, b_ref, sems.at[1]),
    ]
    for copy in copies:
        copy.start()
    sa[ZERO_SLOT] = jnp.zeros(sa.shape[1:], BF)
    c_ref[...] = jnp.zeros_like(c_ref)
    for k, start, count, base in a_parts:
        split_tiles(news[k], start, count, sa, base)
    for k, start, count, base in b_parts:
        split_tiles(news[k], start, count, sb, base)
    for copy in copies:
        copy.wait()
    split_tiles(a_ref, 0, 8, sa, a_slot(0, 0, 0))
    split_tiles(b_ref, 0, 8, sb, b_slot(0, 0))


def first_splits(news, a_parts, b_parts):
    vmem = pl.BlockSpec(memory_space=pltpu.VMEM)
    hbm = pl.BlockSpec(memory_space=pl.ANY)
    own = tuple(pltpu.with_memory_space_constraint(v, pltpu.HBM) for v in news[:2])
    return pl.pallas_call(
        functools.partial(split_kernel, len(news), a_parts, b_parts),
        out_shape=tuple(pltpu.VMEM(*s) for s in STATE),
        in_specs=[hbm] * 2 + [vmem] * (len(news) - 2),
        out_specs=(vmem,) * 3,
        scratch_shapes=[pltpu.VMEM((8, 128, 128), F32)] * 2 + [pltpu.SemaphoreType.DMA((2,))],
        name="first_splits",
        compiler_params=pltpu.CompilerParams(vmem_limit_bytes=8 * 1024 * 1024),
        cost_estimate=pl.CostEstimate(flops=0, bytes_accessed=4_000_000, transcendentals=0),
    )(*own, *news[2:])


def more_splits_kernel(n_in, a_parts, b_parts, *refs):
    news, (sa, sb) = refs[:n_in], refs[n_in + 2 :]
    for k, start, count, base in a_parts:
        split_tiles(news[k], start, count, sa, base)
    for k, start, count, base in b_parts:
        split_tiles(news[k], start, count, sb, base)


def more_splits(news, a_parts, b_parts, state):
    vmem = pl.BlockSpec(memory_space=pltpu.VMEM)
    tiles = tuple(pltpu.with_memory_space_constraint(s, pltpu.VMEM) for s in state[:2])
    news = tuple(pltpu.with_memory_space_constraint(s, pltpu.VMEM) for s in news)
    sa, sb = pl.pallas_call(
        functools.partial(more_splits_kernel, len(news), a_parts, b_parts),
        out_shape=tuple(pltpu.VMEM(*s) for s in STATE[:2]),
        in_specs=[vmem] * (len(news) + 2),
        out_specs=(vmem,) * 2,
        input_output_aliases={len(news) + i: i for i in range(2)},
        name="more_splits",
        compiler_params=pltpu.CompilerParams(vmem_limit_bytes=8 * 1024 * 1024),
        cost_estimate=pl.CostEstimate(flops=0, bytes_accessed=4_000_000, transcendentals=0),
    )(*news, *tiles)
    return sa, sb, state[2]


def products_kernel(stage, a_parts, b_parts, n_in, *refs):
    l_ref = refs[0]
    new = refs[1 : 1 + n_in]
    sa_in, sb_in, c_in = refs[1 + n_in : 4 + n_in]
    sa, sb, c_ref = refs[4 + n_in : 7 + n_in]
    for k, start, count, base in a_parts:
        split_tiles(new[k], start, count, sa, base)
    for k, start, count, base in b_parts:
        split_tiles(new[k], start, count, sb, base)

    def group(size, first):
        sums, places = [], []
        for u in range(size):
            w = l_ref[first + u]
            right = sb[(w >> 8) & 0x3F]
            r = jnp.dot(sa[w & 0xFF], jnp.concatenate([right, right], axis=0), preferred_element_type=F32)
            sums.append(r[:, :128] + r[:, 128:])
            places.append(w >> 14)
        for s, m in zip(sums, places):
            c_ref[m] = c_ref[m] + s

    first = stage * LIST
    left = l_ref[COUNTS + stage]
    for size in GROUPS:
        times = jnp.maximum(left + SMALL - 1, 0) // size

        def step(g, carry, size=size, first=first):
            group(size, first + g * size)
            return carry

        lax.fori_loop(0, times, step, 0)
        first, left = first + times * size, left - times * size
    if stage == CLASSES - 1:
        out_hbm, sem = refs[7 + n_in :]
        copy = pltpu.make_async_copy(c_ref, out_hbm, sem)
        copy.start()
        copy.wait()


def products(stage, entries, news, a_parts, b_parts, state, micros):
    n_in = len(news)
    vmem = pl.BlockSpec(memory_space=pltpu.VMEM)
    smem = pl.BlockSpec(memory_space=pltpu.SMEM)
    state = tuple(pltpu.with_memory_space_constraint(s, pltpu.VMEM) for s in state)
    news = tuple(pltpu.with_memory_space_constraint(s, pltpu.VMEM) for s in news)
    last = stage == CLASSES - 1
    outs = [pltpu.VMEM(*s) for s in STATE]
    aliases = {1 + n_in + i: i for i in range(3)}
    out_specs, scratch = (vmem,) * 3, []
    if last:
        outs += [pltpu.HBM(*STATE[2])]
        out_specs += (pl.BlockSpec(memory_space=pltpu.HBM),)
        scratch = [pltpu.SemaphoreType.DMA(())]
    return pl.pallas_call(
        functools.partial(products_kernel, stage, a_parts, b_parts, n_in),
        out_shape=tuple(outs),
        in_specs=[smem] + [vmem] * (n_in + 3),
        out_specs=out_specs,
        scratch_shapes=scratch,
        input_output_aliases=aliases,
        name=f"products_{stage}",
        compiler_params=pltpu.CompilerParams(vmem_limit_bytes=12 * 1024 * 1024),
        cost_estimate=pl.CostEstimate(flops=5 * 10**10, bytes_accessed=1, transcendentals=0),
    )(entries, *news, *state)


def body(a_tiles, b_tiles, pair_lists, stack_counts):
    barrier = lax.optimization_barrier
    a, b = a_tiles[0, 0], b_tiles[0, 0]
    a10, a03, a01 = move_a(a, dy=1), move_a(a, dx=1), move_a(a, dx=-1)
    words = packed_entries(pair_lists[0, 0], stack_counts[0, 0])
    words, b_late = barrier((words, b))
    b03, b01 = move_b(b_late, dz=1), move_b(b_late, dz=-1)
    entries = sort_entries(words)
    a10, entries, a, b = barrier((a10, entries, a, b))
    b10 = move_b(b, dy=1)
    a13, a11 = move_a(a10, dx=1), move_a(a10, dx=-1)
    state = first_splits(
        (a, b, a10, a03, a01),
        [(2, 0, 8, a_slot(1, 0, 0)), (3, 0, 8, a_slot(0, 3, 0)), (4, 0, 8, a_slot(0, 1, 0))],
        [],
    )
    b03, b01, *state = barrier((b03, b01, *state))
    b02p, b02m = move_b(b03[:4], dz=1), move_b(b01[4:], dz=-1)
    b10, b02p, b02m = barrier((b10, b02p, b02m))
    b13, b11 = move_b(b10, dz=1), move_b(b10, dz=-1)
    state = more_splits(
        (a13, a11, b03, b01, b10, b02p, b02m),
        [(0, 0, 8, a_slot(1, 3, 0)), (1, 0, 8, a_slot(1, 1, 0))],
        [
            (2, 0, 8, b_slot(0, 3)),
            (3, 0, 8, b_slot(0, 1)),
            (4, 0, 8, b_slot(1, 0)),
            (5, 0, 4, b_slot(0, 2)),
            (6, 0, 4, b_slot(0, 2) + 4),
        ],
        state,
    )
    a, a10, a03, a01, a13, a11, *state = barrier((a, a10, a03, a01, a13, a11, *state))
    ap = move_a(jnp.concatenate([a03[:4], a13[:4]]), dx=1)
    am = move_a(jnp.concatenate([a01[4:], a11[4:]]), dx=-1)
    near = move_a(jnp.concatenate([a, a10, a03, a01, a13, a11]), dc=1)
    state = products(0, entries, (), [], [], state, 3)
    state = products(
        1,
        entries,
        (near,),
        [
            (0, 8 * k, 8, a_slot(dy, dx, 1))
            for k, (dy, dx) in enumerate(((0, 0), (1, 0), (0, 3), (0, 1), (1, 3), (1, 1)))
        ],
        [],
        state,
        4,
    )
    b13, b11, *state = barrier((b13, b11, *state))
    b12p, b12m = move_b(b13[:4], dz=1), move_b(b11[4:], dz=-1)
    ap, am, b13, b11 = barrier((ap, am, b13, b11))
    far = move_a(jnp.concatenate([ap, am]), dc=1)
    state = products(
        2,
        entries,
        (ap, am, b13, b11),
        [(h, 4 * dy, 4, a_slot(dy, 2, 0) + 4 * h) for h in (0, 1) for dy in (0, 1)],
        [(2, 0, 8, b_slot(1, 3)), (3, 0, 8, b_slot(1, 1))],
        state,
        3,
    )
    state = products(
        3,
        entries,
        (far,),
        [(0, 8 * h + 4 * dy, 4, a_slot(dy, 2, 1) + 4 * h) for h in (0, 1) for dy in (0, 1)],
        [],
        state,
        3,
    )
    c = products(
        4,
        entries,
        (b12p, b12m),
        [],
        [(h, 0, 4, b_slot(1, 2) + 4 * h) for h in (0, 1)],
        state,
        2,
    )[3]
    return c[None, None]


def solution(mesh):
    return jax.shard_map(
        body,
        mesh=mesh,
        in_specs=(
            P("row", "col", None, None, None),
            P("row", "col", None, None, None),
            P("row", "col", None, None, None),
            P("row", "col", None),
        ),
        out_specs=P("row", "col", None, None, None),
        check_vma=False,
    )
```

```python
import functools

import jax
import jax.numpy as jnp
from jax import lax
from jax.experimental import pallas as pl
from jax.experimental.pallas import tpu as pltpu
from jax.sharding import PartitionSpec as P

CT = 32
GROUPS = (64, 32, 16, 8)
SMALL = 8
CLASSES = 5
LIST = 512 + SMALL
COUNTS = (CLASSES + 1) * LIST
A_SLOTS = 128
ZERO_SLOT = A_SLOTS
B_SLOTS = 64
BF = jnp.bfloat16
F32 = jnp.float32


def move_a(value, dy=0, dx=0, dc=0):
    pairs = []
    for i in range(16):
        y, x, c = i // 8, (i // 2) % 4, i % 2
        pairs.append((i, ((y + dy) % 2) * 8 + ((x + dx) % 4) * 2 + (c + dc) % 2))
    return lax.ppermute(value, "col", pairs)


def move_b(value, dy=0, dz=0):
    pairs = []
    for i in range(8):
        y, z = i // 4, i % 4
        pairs.append((i, ((y + dy) % 2) * 4 + (z + dz) % 4))
    return lax.ppermute(value, "row", pairs)


def a_slot(dy, dx, dc):
    return ((dy * 4 + dx) * 2 + dc) * 8


def b_slot(dy, dz):
    return (dy * 4 + dz) * 8


def stage_of(dy, dx, dc, by, bz):
    far_b = (by == 1) & (bz != 0)
    stage = jnp.where(far_b, 2, dc)
    stage = jnp.where(dx == 2, 3, stage)
    return jnp.where(far_b & (bz == 2), 4, stage)


def packed_entries(lists, counts):
    q = lax.axis_index("col")
    r = lax.axis_index("row")
    j = jnp.arange(16, dtype=jnp.int32)[:, None]
    dy, dx, dc = (j // 8) ^ (q // 8), ((j // 2) - (q // 2)) & 3, (j & 1) ^ (q & 1)
    a, b, m = lists[:, 0], lists[:, 1], lists[:, 2]
    part = b >> 3
    by, bz = (part >> 2) ^ (r >> 2), (part - r) & 3
    stage = stage_of(dy, dx, dc, by, bz)
    live = jnp.arange(32, dtype=jnp.int32)[None, :] < counts[:, None]
    stage = jnp.where(live, stage, CLASSES)
    slot_a = ((dy * 4 + dx) * 2 + dc) * 8 + a
    slot_b = (by * 4 + bz) * 8 + (b & 7)
    return (slot_a | (slot_b << 8) | (m << 14) | (stage << 19)).reshape(-1)


def halves(v):
    hi = v.astype(BF)
    return hi, (v - hi.astype(F32)).astype(BF)


def split_tiles(src, start, count, dst, base):
    def one(i, carry):
        hi, lo = halves(src[start + i])
        dst[base + i, :, :128] = hi
        dst[base + i, :, 128:] = lo
        return carry

    lax.fori_loop(0, count, one, 0, unroll=4)


def sort_kernel(w_ref, words_ref, l_ref, rank_ref, place_ref, counts, places, sems):
    kinds = jnp.broadcast_to(words_ref[...] >> 19, (8, 512))
    is_kind = kinds == lax.broadcasted_iota(jnp.int32, (8, 512), 0)
    before = lax.broadcasted_iota(jnp.int32, (512, 512), 0) <= lax.broadcasted_iota(jnp.int32, (512, 512), 1)
    ones = jnp.where(is_kind, 1.0, 0.0).astype(BF)
    triangle = jnp.where(before, 1.0, 0.0).astype(BF)
    rank = jnp.dot(ones, triangle, preferred_element_type=F32).astype(jnp.int32)
    rank_ref[...] = rank
    starts = lax.broadcasted_iota(jnp.int32, (8, 512), 0) * LIST
    place_ref[...] = jnp.sum(jnp.where(is_kind, starts + rank - 1, 0), axis=0, keepdims=True)
    copies = [
        pltpu.make_async_copy(rank_ref, counts, sems.at[0]),
        pltpu.make_async_copy(place_ref, places, sems.at[1]),
    ]
    for copy in copies:
        copy.start()
    for copy in copies:
        copy.wait()

    def store(e, carry):
        l_ref[places[0, e]] = w_ref[e] & 0x7FFFF
        return carry

    lax.fori_loop(0, 512, store, 0, unroll=16)
    for k in range(CLASSES):
        count = counts[k, 511]
        for u in range(SMALL):
            l_ref[k * LIST + count + u] = jnp.int32(ZERO_SLOT)
        l_ref[COUNTS + k] = count


def sort_entries(words):
    smem = pl.BlockSpec(memory_space=pltpu.SMEM)
    return pl.pallas_call(
        sort_kernel,
        out_shape=jax.ShapeDtypeStruct((COUNTS + CLASSES,), jnp.int32),
        in_specs=[smem, pl.BlockSpec(memory_space=pltpu.VMEM)],
        out_specs=smem,
        scratch_shapes=[
            pltpu.VMEM((8, 512), jnp.int32),
            pltpu.VMEM((1, 512), jnp.int32),
            pltpu.SMEM((8, 512), jnp.int32),
            pltpu.SMEM((1, 512), jnp.int32),
            pltpu.SemaphoreType.DMA((2,)),
        ],
        name="sort_entries",
        cost_estimate=pl.CostEstimate(flops=0, bytes_accessed=16_000_000, transcendentals=0),
    )(words, words.reshape(1, 512))


STATE = (
    ((A_SLOTS + 1, 128, 256), BF),
    ((B_SLOTS, 128, 256), BF),
    ((CT, 128, 128), F32),
)


def split_kernel(n_in, a_parts, b_parts, *refs):
    news, (sa, sb, c_ref) = refs[:n_in], refs[n_in : n_in + 3]
    a_hbm, b_hbm = news[:2]
    a_ref, b_ref, sems = refs[n_in + 3 :]
    copies = [
        pltpu.make_async_copy(a_hbm, a_ref, sems.at[0]),
        pltpu.make_async_copy(b_hbm, b_ref, sems.at[1]),
    ]
    for copy in copies:
        copy.start()
    sa[ZERO_SLOT] = jnp.zeros(sa.shape[1:], BF)
    c_ref[...] = jnp.zeros_like(c_ref)
    for k, start, count, base in a_parts:
        split_tiles(news[k], start, count, sa, base)
    for k, start, count, base in b_parts:
        split_tiles(news[k], start, count, sb, base)
    for copy in copies:
        copy.wait()
    split_tiles(a_ref, 0, 8, sa, a_slot(0, 0, 0))
    split_tiles(b_ref, 0, 8, sb, b_slot(0, 0))


def first_splits(news, a_parts, b_parts):
    vmem = pl.BlockSpec(memory_space=pltpu.VMEM)
    hbm = pl.BlockSpec(memory_space=pl.ANY)
    own = tuple(pltpu.with_memory_space_constraint(v, pltpu.HBM) for v in news[:2])
    return pl.pallas_call(
        functools.partial(split_kernel, len(news), a_parts, b_parts),
        out_shape=tuple(pltpu.VMEM(*s) for s in STATE),
        in_specs=[hbm] * 2 + [vmem] * (len(news) - 2),
        out_specs=(vmem,) * 3,
        scratch_shapes=[pltpu.VMEM((8, 128, 128), F32)] * 2 + [pltpu.SemaphoreType.DMA((2,))],
        name="first_splits",
        compiler_params=pltpu.CompilerParams(vmem_limit_bytes=8 * 1024 * 1024),
        cost_estimate=pl.CostEstimate(flops=0, bytes_accessed=4_000_000, transcendentals=0),
    )(*own, *news[2:])


def more_splits_kernel(n_in, a_parts, b_parts, *refs):
    news, (sa, sb) = refs[:n_in], refs[n_in + 2 :]
    for k, start, count, base in a_parts:
        split_tiles(news[k], start, count, sa, base)
    for k, start, count, base in b_parts:
        split_tiles(news[k], start, count, sb, base)


def more_splits(news, a_parts, b_parts, state):
    vmem = pl.BlockSpec(memory_space=pltpu.VMEM)
    tiles = tuple(pltpu.with_memory_space_constraint(s, pltpu.VMEM) for s in state[:2])
    news = tuple(pltpu.with_memory_space_constraint(s, pltpu.VMEM) for s in news)
    sa, sb = pl.pallas_call(
        functools.partial(more_splits_kernel, len(news), a_parts, b_parts),
        out_shape=tuple(pltpu.VMEM(*s) for s in STATE[:2]),
        in_specs=[vmem] * (len(news) + 2),
        out_specs=(vmem,) * 2,
        input_output_aliases={len(news) + i: i for i in range(2)},
        name="more_splits",
        compiler_params=pltpu.CompilerParams(vmem_limit_bytes=8 * 1024 * 1024),
        cost_estimate=pl.CostEstimate(flops=0, bytes_accessed=4_000_000, transcendentals=0),
    )(*news, *tiles)
    return sa, sb, state[2]


def products_kernel(stage, a_parts, b_parts, n_in, *refs):
    l_ref = refs[0]
    new = refs[1 : 1 + n_in]
    sa_in, sb_in, c_in = refs[1 + n_in : 4 + n_in]
    sa, sb, c_ref = refs[4 + n_in : 7 + n_in]
    for k, start, count, base in a_parts:
        split_tiles(new[k], start, count, sa, base)
    for k, start, count, base in b_parts:
        split_tiles(new[k], start, count, sb, base)

    def group(size, first):
        sums, places = [], []
        for u in range(size):
            w = l_ref[first + u]
            right = sb[(w >> 8) & 0x3F]
            r = jnp.dot(sa[w & 0xFF], jnp.concatenate([right, right], axis=0), preferred_element_type=F32)
            sums.append(r[:, :128] + r[:, 128:])
            places.append(w >> 14)
        for s, m in zip(sums, places):
            c_ref[m] = c_ref[m] + s

    first = stage * LIST
    left = l_ref[COUNTS + stage]
    for size in GROUPS:
        times = jnp.maximum(left + SMALL - 1, 0) // size

        def step(g, carry, size=size, first=first):
            group(size, first + g * size)
            return carry

        lax.fori_loop(0, times, step, 0)
        first, left = first + times * size, left - times * size
    if stage == CLASSES - 1:
        out_hbm, sem = refs[7 + n_in :]
        copy = pltpu.make_async_copy(c_ref, out_hbm, sem)
        copy.start()
        copy.wait()


def products(stage, entries, news, a_parts, b_parts, state, micros):
    n_in = len(news)
    vmem = pl.BlockSpec(memory_space=pltpu.VMEM)
    smem = pl.BlockSpec(memory_space=pltpu.SMEM)
    state = tuple(pltpu.with_memory_space_constraint(s, pltpu.VMEM) for s in state)
    news = tuple(pltpu.with_memory_space_constraint(s, pltpu.VMEM) for s in news)
    last = stage == CLASSES - 1
    outs = [pltpu.VMEM(*s) for s in STATE]
    aliases = {1 + n_in + i: i for i in range(3)}
    out_specs, scratch = (vmem,) * 3, []
    if last:
        outs += [pltpu.HBM(*STATE[2])]
        out_specs += (pl.BlockSpec(memory_space=pltpu.HBM),)
        scratch = [pltpu.SemaphoreType.DMA(())]
    return pl.pallas_call(
        functools.partial(products_kernel, stage, a_parts, b_parts, n_in),
        out_shape=tuple(outs),
        in_specs=[smem] + [vmem] * (n_in + 3),
        out_specs=out_specs,
        scratch_shapes=scratch,
        input_output_aliases=aliases,
        name=f"products_{stage}",
        compiler_params=pltpu.CompilerParams(vmem_limit_bytes=12 * 1024 * 1024),
        cost_estimate=pl.CostEstimate(flops=5 * 10**10, bytes_accessed=1, transcendentals=0),
    )(entries, *news, *state)


def body(a_tiles, b_tiles, pair_lists, stack_counts):
    barrier = lax.optimization_barrier
    a, b = a_tiles[0, 0], b_tiles[0, 0]
    a10 = move_a(a, dy=1)
    words = packed_entries(pair_lists[0, 0], stack_counts[0, 0])
    words, a_late, b_late = barrier((words, a, b))
    a03, a01 = move_a(a_late, dx=1), move_a(a_late, dx=-1)
    b03, b01 = move_b(b_late, dz=1), move_b(b_late, dz=-1)
    entries = sort_entries(words)
    a10, entries, a, b = barrier((a10, entries, a, b))
    b10 = move_b(b, dy=1)
    a13, a11 = move_a(a10, dx=1), move_a(a10, dx=-1)
    state = first_splits(
        (a, b, a10, a03, a01),
        [(2, 0, 8, a_slot(1, 0, 0)), (3, 0, 8, a_slot(0, 3, 0)), (4, 0, 8, a_slot(0, 1, 0))],
        [],
    )
    b03, b01, *state = barrier((b03, b01, *state))
    b02p, b02m = move_b(b03[:4], dz=1), move_b(b01[4:], dz=-1)
    b10, b02p, b02m = barrier((b10, b02p, b02m))
    b13, b11 = move_b(b10, dz=1), move_b(b10, dz=-1)
    state = more_splits(
        (a13, a11, b03, b01, b10, b02p, b02m),
        [(0, 0, 8, a_slot(1, 3, 0)), (1, 0, 8, a_slot(1, 1, 0))],
        [
            (2, 0, 8, b_slot(0, 3)),
            (3, 0, 8, b_slot(0, 1)),
            (4, 0, 8, b_slot(1, 0)),
            (5, 0, 4, b_slot(0, 2)),
            (6, 0, 4, b_slot(0, 2) + 4),
        ],
        state,
    )
    a, a10, a03, a01, a13, a11, *state = barrier((a, a10, a03, a01, a13, a11, *state))
    ap = move_a(jnp.concatenate([a03[:4], a13[:4]]), dx=1)
    am = move_a(jnp.concatenate([a01[4:], a11[4:]]), dx=-1)
    near = move_a(jnp.concatenate([a, a10, a03, a01, a13, a11]), dc=1)
    state = products(0, entries, (), [], [], state, 3)
    state = products(
        1,
        entries,
        (near,),
        [
            (0, 8 * k, 8, a_slot(dy, dx, 1))
            for k, (dy, dx) in enumerate(((0, 0), (1, 0), (0, 3), (0, 1), (1, 3), (1, 1)))
        ],
        [],
        state,
        4,
    )
    b13, b11, *state = barrier((b13, b11, *state))
    b12p, b12m = move_b(b13[:4], dz=1), move_b(b11[4:], dz=-1)
    ap, am, b13, b11 = barrier((ap, am, b13, b11))
    far = move_a(jnp.concatenate([ap, am]), dc=1)
    state = products(
        2,
        entries,
        (ap, am, b13, b11),
        [(h, 4 * dy, 4, a_slot(dy, 2, 0) + 4 * h) for h in (0, 1) for dy in (0, 1)],
        [(2, 0, 8, b_slot(1, 3)), (3, 0, 8, b_slot(1, 1))],
        state,
        3,
    )
    state = products(
        3,
        entries,
        (far,),
        [(0, 8 * h + 4 * dy, 4, a_slot(dy, 2, 1) + 4 * h) for h in (0, 1) for dy in (0, 1)],
        [],
        state,
        3,
    )
    c = products(
        4,
        entries,
        (b12p, b12m),
        [],
        [(h, 0, 4, b_slot(1, 2) + 4 * h) for h in (0, 1)],
        state,
        2,
    )[3]
    return c[None, None]


def solution(mesh):
    return jax.shard_map(
        body,
        mesh=mesh,
        in_specs=(
            P("row", "col", None, None, None),
            P("row", "col", None, None, None),
            P("row", "col", None, None, None),
            P("row", "col", None),
        ),
        out_specs=P("row", "col", None, None, None),
        check_vma=False,
    )
```

```python
import functools

import jax
import jax.numpy as jnp
from jax import lax
from jax.experimental import pallas as pl
from jax.experimental.pallas import tpu as pltpu
from jax.sharding import PartitionSpec as P

CT = 32
GROUPS = (64, 32, 16, 8)
SMALL = 8
CLASSES = 5
LIST = 512 + SMALL
COUNTS = (CLASSES + 1) * LIST
A_SLOTS = 128
ZERO_SLOT = A_SLOTS
B_SLOTS = 64
BF = jnp.bfloat16
F32 = jnp.float32


def move_a(value, dy=0, dx=0, dc=0):
    pairs = []
    for i in range(16):
        y, x, c = i // 8, (i // 2) % 4, i % 2
        pairs.append((i, ((y + dy) % 2) * 8 + ((x + dx) % 4) * 2 + (c + dc) % 2))
    return lax.ppermute(value, "col", pairs)


def move_b(value, dy=0, dz=0):
    pairs = []
    for i in range(8):
        y, z = i // 4, i % 4
        pairs.append((i, ((y + dy) % 2) * 4 + (z + dz) % 4))
    return lax.ppermute(value, "row", pairs)


def a_slot(dy, dx, dc):
    return ((dy * 4 + dx) * 2 + dc) * 8


def b_slot(dy, dz):
    return (dy * 4 + dz) * 8


def stage_of(dy, dx, dc, by, bz):
    far_b = (by == 1) & (bz != 0)
    stage = jnp.where(far_b, 2, dc)
    stage = jnp.where(dx == 2, 3, stage)
    return jnp.where(far_b & (bz == 2), 4, stage)


def packed_entries(lists, live):
    q = lax.axis_index("col")
    r = lax.axis_index("row")
    j = jnp.arange(16, dtype=jnp.int32)[:, None]
    dy, dx, dc = (j // 8) ^ (q // 8), ((j // 2) - (q // 2)) & 3, (j & 1) ^ (q & 1)
    a, b, m = lists[:, 0], lists[:, 1], lists[:, 2]
    part = b >> 3
    by, bz = (part >> 2) ^ (r >> 2), (part - r) & 3
    stage = stage_of(dy, dx, dc, by, bz)
    stage = jnp.where(live, stage, CLASSES)
    slot_a = ((dy * 4 + dx) * 2 + dc) * 8 + a
    slot_b = (by * 4 + bz) * 8 + (b & 7)
    return (slot_a | (slot_b << 8) | (m << 14) | (stage << 19)).reshape(-1)


def halves(v):
    hi = v.astype(BF)
    return hi, (v - hi.astype(F32)).astype(BF)


def split_tiles(src, start, count, dst, base):
    def one(i, carry):
        hi, lo = halves(src[start + i])
        dst[base + i, :, :128] = hi
        dst[base + i, :, 128:] = lo
        return carry

    lax.fori_loop(0, count, one, 0, unroll=4)


def sort_kernel(w_ref, words_ref, l_ref, rank_ref, place_ref, counts, places, sems):
    kinds = jnp.broadcast_to(words_ref[...] >> 19, (8, 512))
    is_kind = kinds == lax.broadcasted_iota(jnp.int32, (8, 512), 0)
    before = lax.broadcasted_iota(jnp.int32, (512, 512), 0) <= lax.broadcasted_iota(jnp.int32, (512, 512), 1)
    ones = jnp.where(is_kind, 1.0, 0.0).astype(BF)
    triangle = jnp.where(before, 1.0, 0.0).astype(BF)
    rank = jnp.dot(ones, triangle, preferred_element_type=F32).astype(jnp.int32)
    rank_ref[...] = rank
    starts = lax.broadcasted_iota(jnp.int32, (8, 512), 0) * LIST
    place_ref[...] = jnp.sum(jnp.where(is_kind, starts + rank - 1, 0), axis=0, keepdims=True)
    copies = [
        pltpu.make_async_copy(rank_ref, counts, sems.at[0]),
        pltpu.make_async_copy(place_ref, places, sems.at[1]),
    ]
    for copy in copies:
        copy.start()
    for copy in copies:
        copy.wait()

    def store(e, carry):
        l_ref[places[0, e]] = w_ref[e] & 0x7FFFF
        return carry

    lax.fori_loop(0, 512, store, 0, unroll=16)
    for k in range(CLASSES):
        count = counts[k, 511]
        for u in range(SMALL):
            l_ref[k * LIST + count + u] = jnp.int32(ZERO_SLOT)
        l_ref[COUNTS + k] = count


def sort_entries(words):
    smem = pl.BlockSpec(memory_space=pltpu.SMEM)
    return pl.pallas_call(
        sort_kernel,
        out_shape=jax.ShapeDtypeStruct((COUNTS + CLASSES,), jnp.int32),
        in_specs=[smem, pl.BlockSpec(memory_space=pltpu.VMEM)],
        out_specs=smem,
        scratch_shapes=[
            pltpu.VMEM((8, 512), jnp.int32),
            pltpu.VMEM((1, 512), jnp.int32),
            pltpu.SMEM((8, 512), jnp.int32),
            pltpu.SMEM((1, 512), jnp.int32),
            pltpu.SemaphoreType.DMA((2,)),
        ],
        name="sort_entries",
        cost_estimate=pl.CostEstimate(flops=0, bytes_accessed=16_000_000, transcendentals=0),
    )(words, words.reshape(1, 512))


STATE = (
    ((A_SLOTS + 1, 128, 256), BF),
    ((B_SLOTS, 128, 256), BF),
    ((CT, 128, 128), F32),
)


def split_kernel(n_in, a_parts, b_parts, *refs):
    news, (sa, sb, c_ref) = refs[:n_in], refs[n_in : n_in + 3]
    a_hbm, b_hbm = news[:2]
    a_ref, b_ref, sems = refs[n_in + 3 :]
    copies = [
        pltpu.make_async_copy(a_hbm, a_ref, sems.at[0]),
        pltpu.make_async_copy(b_hbm, b_ref, sems.at[1]),
    ]
    for copy in copies:
        copy.start()
    sa[ZERO_SLOT] = jnp.zeros(sa.shape[1:], BF)
    c_ref[...] = jnp.zeros_like(c_ref)
    for k, start, count, base in a_parts:
        split_tiles(news[k], start, count, sa, base)
    for k, start, count, base in b_parts:
        split_tiles(news[k], start, count, sb, base)
    for copy in copies:
        copy.wait()
    split_tiles(a_ref, 0, 8, sa, a_slot(0, 0, 0))
    split_tiles(b_ref, 0, 8, sb, b_slot(0, 0))


def first_splits(news, a_parts, b_parts):
    vmem = pl.BlockSpec(memory_space=pltpu.VMEM)
    hbm = pl.BlockSpec(memory_space=pl.ANY)
    own = tuple(pltpu.with_memory_space_constraint(v, pltpu.HBM) for v in news[:2])
    return pl.pallas_call(
        functools.partial(split_kernel, len(news), a_parts, b_parts),
        out_shape=tuple(pltpu.VMEM(*s) for s in STATE),
        in_specs=[hbm] * 2 + [vmem] * (len(news) - 2),
        out_specs=(vmem,) * 3,
        scratch_shapes=[pltpu.VMEM((8, 128, 128), F32)] * 2 + [pltpu.SemaphoreType.DMA((2,))],
        name="first_splits",
        compiler_params=pltpu.CompilerParams(vmem_limit_bytes=8 * 1024 * 1024),
        cost_estimate=pl.CostEstimate(flops=0, bytes_accessed=4_000_000, transcendentals=0),
    )(*own, *news[2:])


def more_splits_kernel(n_in, a_parts, b_parts, *refs):
    news, (sa, sb) = refs[:n_in], refs[n_in + 2 :]
    for k, start, count, base in a_parts:
        split_tiles(news[k], start, count, sa, base)
    for k, start, count, base in b_parts:
        split_tiles(news[k], start, count, sb, base)


def more_splits(news, a_parts, b_parts, state):
    vmem = pl.BlockSpec(memory_space=pltpu.VMEM)
    tiles = tuple(pltpu.with_memory_space_constraint(s, pltpu.VMEM) for s in state[:2])
    news = tuple(pltpu.with_memory_space_constraint(s, pltpu.VMEM) for s in news)
    sa, sb = pl.pallas_call(
        functools.partial(more_splits_kernel, len(news), a_parts, b_parts),
        out_shape=tuple(pltpu.VMEM(*s) for s in STATE[:2]),
        in_specs=[vmem] * (len(news) + 2),
        out_specs=(vmem,) * 2,
        input_output_aliases={len(news) + i: i for i in range(2)},
        name="more_splits",
        compiler_params=pltpu.CompilerParams(vmem_limit_bytes=8 * 1024 * 1024),
        cost_estimate=pl.CostEstimate(flops=0, bytes_accessed=4_000_000, transcendentals=0),
    )(*news, *tiles)
    return sa, sb, state[2]


def products_kernel(stage, a_parts, b_parts, n_in, *refs):
    l_ref = refs[0]
    new = refs[1 : 1 + n_in]
    sa_in, sb_in, c_in = refs[1 + n_in : 4 + n_in]
    sa, sb, c_ref = refs[4 + n_in : 7 + n_in]
    for k, start, count, base in a_parts:
        split_tiles(new[k], start, count, sa, base)
    for k, start, count, base in b_parts:
        split_tiles(new[k], start, count, sb, base)

    def group(size, first):
        sums, places = [], []
        for u in range(size):
            w = l_ref[first + u]
            right = sb[(w >> 8) & 0x3F]
            r = jnp.dot(sa[w & 0xFF], jnp.concatenate([right, right], axis=0), preferred_element_type=F32)
            sums.append(r[:, :128] + r[:, 128:])
            places.append(w >> 14)
        for s, m in zip(sums, places):
            c_ref[m] = c_ref[m] + s

    first = stage * LIST
    left = l_ref[COUNTS + stage]
    for size in GROUPS:
        times = jnp.maximum(left + SMALL - 1, 0) // size

        def step(g, carry, size=size, first=first):
            group(size, first + g * size)
            return carry

        lax.fori_loop(0, times, step, 0)
        first, left = first + times * size, left - times * size
    if stage == CLASSES - 1:
        out_hbm, sem = refs[7 + n_in :]
        copy = pltpu.make_async_copy(c_ref, out_hbm, sem)
        copy.start()
        copy.wait()


def products(stage, entries, news, a_parts, b_parts, state, micros):
    n_in = len(news)
    vmem = pl.BlockSpec(memory_space=pltpu.VMEM)
    smem = pl.BlockSpec(memory_space=pltpu.SMEM)
    state = tuple(pltpu.with_memory_space_constraint(s, pltpu.VMEM) for s in state)
    news = tuple(pltpu.with_memory_space_constraint(s, pltpu.VMEM) for s in news)
    last = stage == CLASSES - 1
    outs = [pltpu.VMEM(*s) for s in STATE]
    aliases = {1 + n_in + i: i for i in range(3)}
    out_specs, scratch = (vmem,) * 3, []
    if last:
        outs += [pltpu.HBM(*STATE[2])]
        out_specs += (pl.BlockSpec(memory_space=pltpu.HBM),)
        scratch = [pltpu.SemaphoreType.DMA(())]
    return pl.pallas_call(
        functools.partial(products_kernel, stage, a_parts, b_parts, n_in),
        out_shape=tuple(outs),
        in_specs=[smem] + [vmem] * (n_in + 3),
        out_specs=out_specs,
        scratch_shapes=scratch,
        input_output_aliases=aliases,
        name=f"products_{stage}",
        compiler_params=pltpu.CompilerParams(vmem_limit_bytes=12 * 1024 * 1024),
        cost_estimate=pl.CostEstimate(flops=5 * 10**10, bytes_accessed=1, transcendentals=0),
    )(entries, *news, *state)


def body(a_tiles, b_tiles, pair_lists, stack_counts):
    barrier = lax.optimization_barrier
    a, b = a_tiles[0, 0], b_tiles[0, 0]
    a10, a03, a01 = move_a(a, dy=1), move_a(a, dx=1), move_a(a, dx=-1)
    live = jnp.arange(32, dtype=jnp.int32)[None, :] < stack_counts[0, 0][:, None]
    words = packed_entries(pair_lists[0, 0], barrier(live))
    words, b_late = barrier((words, b))
    b03, b01 = move_b(b_late, dz=1), move_b(b_late, dz=-1)
    entries = sort_entries(words)
    a10, entries, a, b = barrier((a10, entries, a, b))
    b10 = move_b(b, dy=1)
    a13, a11 = move_a(a10, dx=1), move_a(a10, dx=-1)
    state = first_splits(
        (a, b, a10, a03, a01),
        [(2, 0, 8, a_slot(1, 0, 0)), (3, 0, 8, a_slot(0, 3, 0)), (4, 0, 8, a_slot(0, 1, 0))],
        [],
    )
    b03, b01, *state = barrier((b03, b01, *state))
    b02p, b02m = move_b(b03[:4], dz=1), move_b(b01[4:], dz=-1)
    b10, b02p, b02m = barrier((b10, b02p, b02m))
    b13, b11 = move_b(b10, dz=1), move_b(b10, dz=-1)
    state = more_splits(
        (a13, a11, b03, b01, b10, b02p, b02m),
        [(0, 0, 8, a_slot(1, 3, 0)), (1, 0, 8, a_slot(1, 1, 0))],
        [
            (2, 0, 8, b_slot(0, 3)),
            (3, 0, 8, b_slot(0, 1)),
            (4, 0, 8, b_slot(1, 0)),
            (5, 0, 4, b_slot(0, 2)),
            (6, 0, 4, b_slot(0, 2) + 4),
        ],
        state,
    )
    a, a10, a03, a01, a13, a11, *state = barrier((a, a10, a03, a01, a13, a11, *state))
    ap = move_a(jnp.concatenate([a03[:4], a13[:4]]), dx=1)
    am = move_a(jnp.concatenate([a01[4:], a11[4:]]), dx=-1)
    near = move_a(jnp.concatenate([a, a10, a03, a01, a13, a11]), dc=1)
    state = products(0, entries, (), [], [], state, 3)
    state = products(
        1,
        entries,
        (near,),
        [
            (0, 8 * k, 8, a_slot(dy, dx, 1))
            for k, (dy, dx) in enumerate(((0, 0), (1, 0), (0, 3), (0, 1), (1, 3), (1, 1)))
        ],
        [],
        state,
        4,
    )
    b13, b11, *state = barrier((b13, b11, *state))
    b12p, b12m = move_b(b13[:4], dz=1), move_b(b11[4:], dz=-1)
    ap, am, b13, b11 = barrier((ap, am, b13, b11))
    far = move_a(jnp.concatenate([ap, am]), dc=1)
    state = products(
        2,
        entries,
        (ap, am, b13, b11),
        [(h, 4 * dy, 4, a_slot(dy, 2, 0) + 4 * h) for h in (0, 1) for dy in (0, 1)],
        [(2, 0, 8, b_slot(1, 3)), (3, 0, 8, b_slot(1, 1))],
        state,
        3,
    )
    state = products(
        3,
        entries,
        (far,),
        [(0, 8 * h + 4 * dy, 4, a_slot(dy, 2, 1) + 4 * h) for h in (0, 1) for dy in (0, 1)],
        [],
        state,
        3,
    )
    c = products(
        4,
        entries,
        (b12p, b12m),
        [],
        [(h, 0, 4, b_slot(1, 2) + 4 * h) for h in (0, 1)],
        state,
        2,
    )[3]
    return c[None, None]


def solution(mesh):
    return jax.shard_map(
        body,
        mesh=mesh,
        in_specs=(
            P("row", "col", None, None, None),
            P("row", "col", None, None, None),
            P("row", "col", None, None, None),
            P("row", "col", None),
        ),
        out_specs=P("row", "col", None, None, None),
        check_vma=False,
    )
```
